32 devices in a mesh: dp: 4 (over y, x), fsdp: 8 (over z, core).
Axes of the slice: x: 2, y: 2, z: 4, core: 2. Of those that a mesh axis runs over, the one named last changes fastest.
Arguments:
- hidden_in: bfloat16 [32768, 1024], P(('dp', 'fsdp')), may hold values from -6 to 6
- text_states: bfloat16 [16384, 1024], P(('dp', 'fsdp')), may hold values from -6 to 6
- long_item: int32 [32], P(('dp', 'fsdp')), may hold values from 0 to 1
- text_slot: int32 [32, 4], P(('dp', 'fsdp')), may hold values from 0 to 3, each once within a row
- out_grad: bfloat16 [32768, 1024], P(('dp', 'fsdp')), may hold values from -6 to 6
- self_gain: bfloat16 [1024], P(('dp', 'fsdp')), may hold values from 0.099609375 to 1.8984375
- self_query: bfloat16 [1024, 1024], P(('dp', 'fsdp')), may hold values from -0.1875 to 0.1875
- self_key: bfloat16 [1024, 1024], P(('dp', 'fsdp')), may hold values from -0.1875 to 0.1875
- self_value: bfloat16 [1024, 1024], P(('dp', 'fsdp')), may hold values from -0.1875 to 0.1875
- self_out: bfloat16 [1024, 1024], P(('dp', 'fsdp')), may hold values from -0.75 to 0.75
- cross_gain: bfloat16 [1024], P(('dp', 'fsdp')), may hold values from 0.099609375 to 1.8984375
- cross_query: bfloat16 [1024, 1024], P(('dp', 'fsdp')), may hold values from -0.1875 to 0.1875
- cross_key: bfloat16 [1024, 1024], P(('dp', 'fsdp')), may hold values from -0.1875 to 0.1875
- cross_value: bfloat16 [1024, 1024], P(('dp', 'fsdp')), may hold values from -0.1875 to 0.1875
- cross_out: bfloat16 [1024, 1024], P(('dp', 'fsdp')), may hold values from -0.75 to 0.75
- mlp_gain: bfloat16 [1024], P(('dp', 'fsdp')), may hold values from 0.099609375 to 1.8984375
- mlp_in: bfloat16 [1024, 4096], P(('dp', 'fsdp')), may hold values from -0.1875 to 0.1875
- mlp_in_bias: bfloat16 [4096], P(('dp', 'fsdp')), may hold values from -3 to 3
- mlp_out: bfloat16 [4096, 1024], P(('dp', 'fsdp')), may hold values from -0.09375 to 0.09375
- mlp_out_bias: bfloat16 [1024], P(('dp', 'fsdp')), may hold values from -3 to 3
Outputs:
- block_out: bfloat16 [32768, 1024], P(('dp', 'fsdp'))
- hidden_grad: float32 [32768, 1024], P(('dp', 'fsdp'))
- text_grad: float32 [16384, 1024], P(('dp', 'fsdp'))
- self_gain_grad: float32 [1024], P(('dp', 'fsdp'))
- self_query_grad: float32 [1024, 1024], P(('dp', 'fsdp'))
- self_key_grad: float32 [1024, 1024], P(('dp', 'fsdp'))
- self_value_grad: float32 [1024, 1024], P(('dp', 'fsdp'))
- self_out_grad: float32 [1024, 1024], P(('dp', 'fsdp'))
- cross_gain_grad: float32 [1024], P(('dp', 'fsdp'))
- cross_query_grad: float32 [1024, 1024], P(('dp', 'fsdp'))
- cross_key_grad: float32 [1024, 1024], P(('dp', 'fsdp'))
- cross_value_grad: float32 [1024, 1024], P(('dp', 'fsdp'))
- cross_out_grad: float32 [1024, 1024], P(('dp', 'fsdp'))
- mlp_gain_grad: float32 [1024], P(('dp', 'fsdp'))
- mlp_in_grad: float32 [1024, 4096], P(('dp', 'fsdp'))
- mlp_in_bias_grad: float32 [4096], P(('dp', 'fsdp'))
- mlp_out_grad: float32 [4096, 1024], P(('dp', 'fsdp'))
- mlp_out_bias_grad: float32 [1024], P(('dp', 'fsdp'))
The draws below stay inside these ranges and needn't reach their ends.
Inputs may be any that keep to these rules, and one draw needn't show every extreme that they name: `long_item`: 1 where the bucket holds one item of 1024 tokens, 0 where it holds 4 items of 256 tokens. Each row is a permutation of the bucket's 4 text blocks; item j of bucket b reads block text_slot[b, j].
All inputs are finite; a program needn't handle non-finite values.
Results may differ from the reference program's by a relative error of at most 0.019.
Values may be sent and summed in bfloat16 or wider, within the bound.
No kernel may reach another device: no remote copies, remote signals or barrier semaphores. Data moves between devices by JAX's collectives and lax.ppermute only.
A program may use at most 320 MiB of HBM per device.

```python
import jax
import jax.numpy as jnp
from jax import lax

D = 1024
HEADS = 16
HEAD_DIM = 64
FF = 4096
ENC = 128
SLOTS = 4
TOK_DEV = 1024
ITEM_SHORT = 256
BUCKETS = 32
TOKENS = 32768
TEXT_ROWS = 16384


def set_ends(values, stream_key, low, largest):
    place = [jax.random.randint(jax.random.fold_in(stream_key, axis), (), 0, length) for axis, length in enumerate(values.shape)]
    widest = values.shape.index(max(values.shape))
    neighbour = place[:widest] + [(place[widest] + 1) % values.shape[widest]] + place[widest + 1:]
    return values.at[tuple(place)].set(low).at[tuple(neighbour)].set(largest)


def block_levels(stream_key, extent, cuts, least, largest):
    def one(dim, shards_of):
        steps = jax.random.uniform(jax.random.fold_in(jax.random.fold_in(stream_key, 6), dim), (shards_of,), jnp.float32, least / len(cuts), largest / len(cuts))
        return jnp.repeat(jnp.exp(steps), extent[dim] // shards_of).reshape((-1,) + (1,) * (len(extent) - dim - 1))

    level = one(*cuts[0])
    for cut in cuts[1:]:
        level = level * one(*cut)
    return level


def gaussian(key, shape, width, most, cuts=(), kind=jnp.bfloat16):
    level = block_levels(key, shape, cuts, -0.22, 0.18) if cuts else 1.0
    result = jax.random.normal(key, shape, jnp.float32) * width * level
    return jnp.minimum(jnp.maximum(result, -most), most).astype(kind)


def setup_inputs(seed: int = 0) -> dict:
    key_of = jax.random.split(jax.random.key(seed), 21)
    hidden_in = gaussian(key_of[0], (TOKENS, D), 1.0, 6.0, ((0, 32),))
    text_states = gaussian(key_of[1], (TEXT_ROWS, D), 1.0, 6.0, ((0, 32),))
    long_item = set_ends(jax.random.randint(key_of[2], (BUCKETS,), 0, 2), jax.random.fold_in(key_of[2], 1), 0, 1).astype(jnp.int32)
    text_slot = jax.vmap(lambda own: jax.random.permutation(own, SLOTS))(jax.random.split(key_of[3], BUCKETS)).reshape((BUCKETS, SLOTS)).astype(jnp.int32)
    out_grad = gaussian(key_of[4], (TOKENS, D), 1.0, 6.0, ((0, 32),))
    self_gain = jnp.clip(1.0 + 0.18 * jax.random.normal(key_of[5], (D,), jnp.float32), 0.099609375, 1.8984375).astype(jnp.bfloat16)
    self_query = gaussian(key_of[6], (D, D), D ** -0.5, 0.1875, ((0, 32),))
    self_key = gaussian(key_of[7], (D, D), D ** -0.5, 0.1875, ((0, 32),))
    self_value = gaussian(key_of[8], (D, D), D ** -0.5, 0.1875, ((0, 32),))
    self_out = gaussian(key_of[9], (D, D), (D // 16) ** -0.5, 0.75, ((0, 32),))
    cross_gain = jnp.clip(1.0 + 0.18 * jax.random.normal(key_of[10], (D,), jnp.float32), 0.099609375, 1.8984375).astype(jnp.bfloat16)
    cross_query = gaussian(key_of[11], (D, D), D ** -0.5, 0.1875, ((0, 32),))
    cross_key = gaussian(key_of[12], (D, D), D ** -0.5, 0.1875, ((0, 32),))
    cross_value = gaussian(key_of[13], (D, D), D ** -0.5, 0.1875, ((0, 32),))
    cross_out = gaussian(key_of[14], (D, D), (D // 16) ** -0.5, 0.75, ((0, 32),))
    mlp_gain = jnp.clip(1.0 + 0.18 * jax.random.normal(key_of[15], (D,), jnp.float32), 0.099609375, 1.8984375).astype(jnp.bfloat16)
    mlp_in = gaussian(key_of[16], (D, FF), D ** -0.5, 0.1875, ((0, 32),))
    mlp_in_bias = gaussian(key_of[17], (FF,), 0.5, 3.0, ((0, 32),))
    mlp_out = gaussian(key_of[18], (FF, D), FF ** -0.5, 0.09375, ((0, 32),))
    mlp_out_bias = gaussian(key_of[19], (D,), 0.5, 3.0, ((0, 32),))
    return {"hidden_in": hidden_in, "text_states": text_states, "long_item": long_item, "text_slot": text_slot, "out_grad": out_grad, "self_gain": self_gain, "self_query": self_query, "self_key": self_key, "self_value": self_value, "self_out": self_out, "cross_gain": cross_gain, "cross_query": cross_query, "cross_key": cross_key, "cross_value": cross_value, "cross_out": cross_out, "mlp_gain": mlp_gain, "mlp_in": mlp_in, "mlp_in_bias": mlp_in_bias, "mlp_out": mlp_out, "mlp_out_bias": mlp_out_bias}


@jax.custom_vjp
def low(v):
    return lax.optimization_barrier(v.astype(jnp.bfloat16)).astype(jnp.float32)

@jax.custom_vjp
def low_back(v):
    return v

def low_keep(v):
    return (low(v), None)

def low_pass(kept, grad):
    return (grad,)

def back_keep(v):
    return (v, None)

def back_low(kept, grad):
    return (low(grad),)
low.defvjp(low_keep, low_pass)
low_back.defvjp(back_keep, back_low)
EPSILON = 1e-05
NEGATIVE = -1000000000.0
SCORE_SCALE = 0.125

def both_round(values):
    return low_back(low(values))

def matmul(first_op, second_op):
    return jnp.dot(first_op, second_op, precision=lax.Precision.HIGHEST)

def layer_norm(values, scales):
    average = lax.optimization_barrier(jnp.mean(values, axis=-1, keepdims=True))
    centred = values - average
    variance = lax.optimization_barrier(jnp.mean(centred * centred, axis=-1, keepdims=True))
    return centred * lax.rsqrt(variance + EPSILON) * scales

def attention(queries, key_rows, value_rows, allowed):
    token_count = queries.shape[0]
    source_count = key_rows.shape[0]
    head_queries = queries.reshape(token_count, HEADS, HEAD_DIM)
    head_keys = key_rows.reshape(source_count, HEADS, HEAD_DIM)
    head_values = value_rows.reshape(source_count, HEADS, HEAD_DIM)
    scores = low_back(SCORE_SCALE * jnp.einsum('thd,shd->hts', head_queries, head_keys, precision=lax.Precision.HIGHEST))
    weights = jax.nn.softmax(jnp.where(allowed[None], scores, NEGATIVE), axis=-1)
    mixture = jnp.einsum('hts,shd->thd', low(weights), head_values, precision=lax.Precision.HIGHEST)
    return mixture.reshape(token_count, D)

def bucket_forward(params, hidden, states, long_flag, slot_row):
    self_gain, self_query, self_key, self_value, self_out, cross_gain, cross_query, cross_key, cross_value, cross_out, mlp_gain, mlp_in, mlp_in_bias, mlp_out, mlp_out_bias = params
    positions = jnp.arange(TOK_DEV, dtype=jnp.int32)
    item_of = jnp.where(long_flag > 0, 0, positions // ITEM_SHORT).astype(jnp.int32)
    slot_ids = jnp.arange(SLOTS, dtype=jnp.int32)
    token_slot = lax.optimization_barrier(jnp.sum(jnp.where(item_of[:, None] == slot_ids[None, :], slot_row[None, :], 0), axis=1)).astype(jnp.int32)
    self_allowed = (item_of[:, None] == item_of[None, :]) & (positions[None, :] <= positions[:, None])
    text_block = (jnp.arange(SLOTS * ENC, dtype=jnp.int32) // ENC).astype(jnp.int32)
    cross_allowed = text_block[None, :] == token_slot[:, None]
    normed_one = low(layer_norm(hidden, self_gain))
    queries_one = both_round(matmul(normed_one, self_query))
    keys_one = both_round(matmul(normed_one, self_key))
    values_one = both_round(matmul(normed_one, self_value))
    mixture_one = both_round(attention(queries_one, keys_one, values_one, self_allowed))
    after_self = hidden + low_back(matmul(mixture_one, self_out))
    normed_two = low(layer_norm(after_self, cross_gain))
    queries_two = both_round(matmul(normed_two, cross_query))
    keys_two = both_round(matmul(states, cross_key))
    values_two = both_round(matmul(states, cross_value))
    mixture_two = both_round(attention(queries_two, keys_two, values_two, cross_allowed))
    after_cross = after_self + low_back(matmul(mixture_two, cross_out))
    normed_three = low(layer_norm(after_cross, mlp_gain))
    before = low_back(matmul(normed_three, mlp_in) + mlp_in_bias)
    active = low(jax.nn.gelu(before))
    return after_cross + matmul(active, mlp_out) + mlp_out_bias

def reference(hidden_in, text_states, long_item, text_slot, out_grad, self_gain, self_query, self_key, self_value, self_out, cross_gain, cross_query, cross_key, cross_value, cross_out, mlp_gain, mlp_in, mlp_in_bias, mlp_out, mlp_out_bias):
    params = tuple((tensor.astype(jnp.float32) for tensor in (self_gain, self_query, self_key, self_value, self_out, cross_gain, cross_query, cross_key, cross_value, cross_out, mlp_gain, mlp_in, mlp_in_bias, mlp_out, mlp_out_bias)))
    hidden = hidden_in.astype(jnp.float32).reshape(BUCKETS, TOK_DEV, D)
    states = text_states.astype(jnp.float32).reshape(BUCKETS, SLOTS * ENC, D)

    def forward_all(weights_all, hidden_all, states_all):

        def one_bucket(pieces):
            return bucket_forward(weights_all, pieces[0], pieces[1], pieces[2], pieces[3])
        return lax.map(jax.checkpoint(one_bucket), (hidden_all, states_all, long_item, text_slot))
    outputs, backward = jax.vjp(forward_all, params, hidden, states)
    param_grads, hidden_grad, text_grad = backward(out_grad.astype(jnp.float32).reshape(BUCKETS, TOK_DEV, D))
    return (outputs.reshape(TOKENS, D).astype(jnp.bfloat16), hidden_grad.reshape(TOKENS, D), text_grad.reshape(TEXT_ROWS, D), param_grads[0], param_grads[1], param_grads[2], param_grads[3], param_grads[4], param_grads[5], param_grads[6], param_grads[7], param_grads[8], param_grads[9], param_grads[10], param_grads[11], param_grads[12], param_grads[13], param_grads[14])
```

```python
import jax
import jax.numpy as jnp
from jax import lax
from jax.sharding import PartitionSpec as P

HEADS = 16


EPSILON = 1e-05
NEGATIVE = -1000000000.0
SCORE_SCALE = 0.125
BLOCK_ROWS = 512


def layer_norm(values, scales):
    average = jnp.mean(values, axis=-1, keepdims=True)
    centred = values - average
    inverse = lax.rsqrt(jnp.mean(centred * centred, axis=-1, keepdims=True) + EPSILON)
    normed = centred * inverse
    return (normed * scales, normed, inverse)


def norm_back(grad_out, normed, inverse, scales):
    scaled = grad_out * scales
    grad_in = inverse * (
        scaled
        - jnp.mean(scaled, axis=-1, keepdims=True)
        - normed * jnp.mean(scaled * normed, axis=-1, keepdims=True)
    )
    return (grad_in, jnp.sum(grad_out * normed, axis=0))


def product(first_op, second_op):
    return jnp.dot(first_op, second_op, preferred_element_type=jnp.float32)


def product_left(first_op, second_op):
    return lax.dot_general(
        first_op, second_op, (((0,), (0,)), ((), ())), preferred_element_type=jnp.float32
    )


def product_right(first_op, second_op):
    return lax.dot_general(
        first_op, second_op, (((1,), (1,)), ((), ())), preferred_element_type=jnp.float32
    )


def split_heads(values):
    return values.reshape(values.shape[0], HEADS, values.shape[1] // HEADS)


def attend(queries, key_rows, value_rows, allowed):
    scores = (
        jnp.einsum(
            "rhd,shd->hrs",
            split_heads(queries),
            split_heads(key_rows),
            preferred_element_type=jnp.float32,
        )
        * SCORE_SCALE
    )
    masked = jnp.where(allowed[None], scores, NEGATIVE)
    highest = jnp.max(masked, axis=-1, keepdims=True)
    weights = jnp.exp(masked - highest)
    summed = jnp.sum(weights, axis=-1, keepdims=True)
    probs_low = (weights / summed).astype(jnp.bfloat16)
    mixture = jnp.einsum(
        "hrs,shd->rhd", probs_low, split_heads(value_rows), preferred_element_type=jnp.float32
    )
    return (mixture.reshape(queries.shape), (highest + jnp.log(summed))[..., 0])


def attend_back(queries, key_rows, value_rows, allowed, log_total, grad_mix):
    head_queries = split_heads(queries)
    head_keys = split_heads(key_rows)
    head_values = split_heads(value_rows)
    head_grad = split_heads(grad_mix)
    scores = (
        jnp.einsum("rhd,shd->hrs", head_queries, head_keys, preferred_element_type=jnp.float32)
        * SCORE_SCALE
    )
    masked = jnp.where(allowed[None], scores, NEGATIVE)
    weights = jnp.exp(masked - log_total[..., None])
    grad_weights = jnp.einsum(
        "rhd,shd->hrs", head_grad, head_values, preferred_element_type=jnp.float32
    )
    row_dot = jnp.sum(weights * grad_weights, axis=-1, keepdims=True)
    grad_scores = (weights * (grad_weights - row_dot)).astype(jnp.bfloat16)
    grad_queries = (
        jnp.einsum("hrs,shd->rhd", grad_scores, head_keys, preferred_element_type=jnp.float32)
        * SCORE_SCALE
    )
    grad_keys = (
        jnp.einsum("hrs,rhd->shd", grad_scores, head_queries, preferred_element_type=jnp.float32)
        * SCORE_SCALE
    )
    grad_values = jnp.einsum(
        "hrs,rhd->shd", weights.astype(jnp.bfloat16), head_grad, preferred_element_type=jnp.float32
    )
    return (
        grad_queries.reshape(queries.shape),
        grad_keys.reshape(key_rows.shape),
        grad_values.reshape(value_rows.shape),
    )

AXES = ("dp", "fsdp")


def bits_of(count):
    return [1 << step for step in range(count.bit_length() - 1)]


def swap(values, axis, bit):
    count = lax.axis_size(axis)
    return lax.ppermute(values, axis, [(place, place ^ bit) for place in range(count)])


def stage_order(flip):
    across = [("dp", bit) for bit in bits_of(lax.axis_size("dp"))]
    along = [("fsdp", bit) for bit in bits_of(lax.axis_size("fsdp"))]
    if flip:
        across = across[::-1]
    return along[:1] + across + along[1:]


def reduce_shards(values, flip=False):
    dims = [("dp", bit) for bit in bits_of(lax.axis_size("dp"))[::-1]]
    dims += [("fsdp", bit) for bit in bits_of(lax.axis_size("fsdp"))[::-1]]
    kind = values.dtype
    values = values.reshape((2,) * len(dims) + values.shape[1:])
    for axis, bit in stage_order(flip):
        place = dims.index((axis, bit))
        own = jnp.where((lax.axis_index(axis) & bit) != 0, 1, 0)
        sent = lax.dynamic_index_in_dim(values, 1 - own, place, keepdims=False)
        kept = lax.dynamic_index_in_dim(values, own, place, keepdims=False)
        received = swap(sent, axis, bit)
        del dims[place]
        total = kept.astype(jnp.float32) + received.astype(jnp.float32)
        values = total.astype(kind) if dims else total
    return values


def by_owner(values):
    owners = lax.axis_size("dp") * lax.axis_size("fsdp")
    return values.reshape((owners, values.shape[0] // owners) + values.shape[1:])


def gather(values):
    return lax.all_gather(values, AXES, axis=0, tiled=True)


def self_mask(positions, item_of, row_begin, row_end):
    return (item_of[row_begin:row_end, None] == item_of[None, :row_end]) & (
        positions[None, :row_end] <= positions[row_begin:row_end, None]
    )


def cross_groups(item_of, token_slot, row_begin, row_end, item_len, text_len):
    lead_rows = list(range(row_begin, row_end, item_len))
    masks = []
    offsets = []
    for group_idx, lead_row in enumerate(lead_rows):
        allowed = item_of[row_begin:row_end] == item_of[lead_row]
        if group_idx > 0:
            allowed = allowed & (item_of[lead_row] != item_of[lead_rows[group_idx - 1]])
        masks.append(jnp.broadcast_to(allowed[:, None], (row_end - row_begin, text_len)))
        offsets.append(token_slot[lead_row] * text_len)
    return (jnp.concatenate(masks, axis=1), offsets)


def text_rows_for(source, offsets, text_len):
    return jnp.concatenate(
        [lax.dynamic_slice_in_dim(source, offset, text_len, 0) for offset in offsets], axis=0
    )


def add_rows(accumulator, part_rows, offset):
    length = part_rows.shape[0]
    current = lax.dynamic_slice_in_dim(accumulator, offset, length, 0)
    return lax.dynamic_update_slice_in_dim(accumulator, current + part_rows, offset, 0)


def local(
    hidden_in,
    text_states,
    long_item,
    text_slot,
    out_grad,
    self_gain,
    self_query,
    self_key,
    self_value,
    self_out,
    cross_gain,
    cross_query,
    cross_key,
    cross_value,
    cross_out,
    mlp_gain,
    mlp_in,
    mlp_in_bias,
    mlp_out,
    mlp_out_bias,
):
    token_count = hidden_in.shape[0]
    slot_count = text_slot.shape[1]
    text_len = text_states.shape[0] // slot_count
    item_len = token_count // slot_count
    block_len = min(BLOCK_ROWS, token_count)
    blocks = [(start_row, start_row + block_len) for start_row in range(0, token_count, block_len)]
    positions = jnp.arange(token_count, dtype=jnp.int32)
    item_of = jnp.where(long_item[0] > 0, 0, positions // item_len)
    slot_ids = jnp.arange(slot_count, dtype=jnp.int32)
    token_slot = jnp.sum(
        jnp.where(item_of[:, None] == slot_ids[None, :], text_slot[0][None, :], 0), axis=1
    )
    width = hidden_in.shape[1]
    own_rows = self_query.shape[0]
    small = jnp.concatenate([self_gain, cross_gain, mlp_gain, mlp_in_bias, mlp_out_bias])
    small_rows = -(-small.shape[0] // 128)
    small = jnp.pad(small, (0, small_rows * 128 - small.shape[0])).reshape(small_rows, 128)
    small = jnp.pad(small, ((0, own_rows - small_rows), (0, 0)))
    first = gather(jnp.concatenate([self_query, self_key, self_value, small], axis=1))
    first, later = lax.optimization_barrier(
        (first, (self_out, cross_query, cross_key, cross_value, cross_out))
    )
    second = gather(jnp.concatenate(later, axis=1))
    out_parts = mlp_out.reshape(-1, own_rows, width)
    part_count = out_parts.shape[0]
    second, later = lax.optimization_barrier((second, (mlp_in, out_parts)))
    third = gather(
        jnp.concatenate([later[0]] + [later[1][part] for part in range(part_count)], axis=1)
    )
    qkv_self = first[:, : 3 * width]
    spread = first[:, 3 * width :].reshape(-1, own_rows, 128)[:, :small_rows].reshape(-1, small_rows * 128)
    cuts = [0]
    for tensor in (self_gain, cross_gain, mlp_gain, mlp_in_bias, mlp_out_bias):
        cuts.append(cuts[-1] + tensor.shape[0])
    gain_self, gain_cross, gain_mlp, bias_in, bias_out = (
        spread[:, low:high].reshape(-1) for low, high in zip(cuts[:-1], cuts[1:])
    )
    out_self, query_cross, key_cross, value_cross, out_cross = (
        second[:, place * width : (place + 1) * width] for place in range(5)
    )
    in_mlp = third[:, : mlp_in.shape[1]]
    out_mlp = (
        third[:, mlp_in.shape[1] :]
        .reshape(-1, own_rows, part_count, width)
        .transpose(0, 2, 1, 3)
        .reshape(-1, width)
    )
    hidden = hidden_in.astype(jnp.float32)
    normed_one, plain_one, inverse_one = layer_norm(hidden, gain_self.astype(jnp.float32))
    input_one = normed_one.astype(jnp.bfloat16)
    qkv_one = product(input_one, qkv_self).astype(jnp.bfloat16)
    queries_one = qkv_one[:, :width]
    keys_one = qkv_one[:, width : 2 * width]
    values_one = qkv_one[:, 2 * width :]
    mixtures = []
    totals_one = []
    for row_begin, row_end in blocks:
        allowed = self_mask(positions, item_of, row_begin, row_end)
        mixture, log_total = attend(
            queries_one[row_begin:row_end], keys_one[:row_end], values_one[:row_end], allowed
        )
        mixtures.append(mixture)
        totals_one.append(log_total)
    mixture_one = jnp.concatenate(mixtures, axis=0).astype(jnp.bfloat16)
    after_self = hidden + product(mixture_one, out_self)
    normed_two, plain_two, inverse_two = layer_norm(after_self, gain_cross.astype(jnp.float32))
    input_two = normed_two.astype(jnp.bfloat16)
    queries_two = product(input_two, query_cross).astype(jnp.bfloat16)
    keys_two = product(text_states, key_cross).astype(jnp.bfloat16)
    values_two = product(text_states, value_cross).astype(jnp.bfloat16)
    mixtures = []
    totals_two = []
    for row_begin, row_end in blocks:
        allowed, offsets = cross_groups(item_of, token_slot, row_begin, row_end, item_len, text_len)
        mixture, log_total = attend(
            queries_two[row_begin:row_end],
            text_rows_for(keys_two, offsets, text_len),
            text_rows_for(values_two, offsets, text_len),
            allowed,
        )
        mixtures.append(mixture)
        totals_two.append(log_total)
    mixture_two = jnp.concatenate(mixtures, axis=0).astype(jnp.bfloat16)
    after_cross = after_self + product(mixture_two, out_cross)
    normed_three, plain_three, inverse_three = layer_norm(after_cross, gain_mlp.astype(jnp.float32))
    input_three = normed_three.astype(jnp.bfloat16)
    before = product(input_three, in_mlp) + bias_in.astype(jnp.float32)
    active_low = jax.nn.gelu(before).astype(jnp.bfloat16)
    block_out = (after_cross + product(active_low, out_mlp) + bias_out.astype(jnp.float32)).astype(
        jnp.bfloat16
    )
    grad_top = out_grad.astype(jnp.float32)
    grad_bias_out = jnp.sum(grad_top, axis=0)
    grad_out_mlp = product_left(active_low, out_grad)
    grad_active = product_right(out_grad, out_mlp)
    grad_before = jax.vjp(jax.nn.gelu, before)[1](grad_active)[0].astype(jnp.bfloat16)
    grad_bias_in = jnp.sum(grad_before.astype(jnp.float32), axis=0)
    grad_in_mlp = product_left(input_three, grad_before)
    grad_part, grad_gain_mlp = norm_back(
        product_right(grad_before, in_mlp), plain_three, inverse_three, gain_mlp.astype(jnp.float32)
    )
    grad_cross = grad_top + grad_part
    shard_out_mlp = reduce_shards(by_owner(grad_out_mlp.astype(jnp.bfloat16)))
    shard_in_mlp = reduce_shards(by_owner(grad_in_mlp.astype(jnp.bfloat16)), True)
    grad_low_two = grad_cross.astype(jnp.bfloat16)
    grad_out_cross = product_left(mixture_two, grad_low_two)
    grad_mix_two = product_right(grad_low_two, out_cross).astype(jnp.bfloat16)
    query_parts = []
    grad_keys_two = jnp.zeros(keys_two.shape, jnp.float32)
    grad_values_two = jnp.zeros(values_two.shape, jnp.float32)
    for (row_begin, row_end), log_total in zip(blocks, totals_two):
        allowed, offsets = cross_groups(item_of, token_slot, row_begin, row_end, item_len, text_len)
        block_q_grad, block_k_grad, block_v_grad = attend_back(
            queries_two[row_begin:row_end],
            text_rows_for(keys_two, offsets, text_len),
            text_rows_for(values_two, offsets, text_len),
            allowed,
            log_total,
            grad_mix_two[row_begin:row_end],
        )
        query_parts.append(block_q_grad)
        for group_idx, offset in enumerate(offsets):
            grad_keys_two = add_rows(
                grad_keys_two,
                block_k_grad[group_idx * text_len : (group_idx + 1) * text_len],
                offset,
            )
            grad_values_two = add_rows(
                grad_values_two,
                block_v_grad[group_idx * text_len : (group_idx + 1) * text_len],
                offset,
            )
    grad_queries_two = jnp.concatenate(query_parts, axis=0).astype(jnp.bfloat16)
    grad_keys_low = grad_keys_two.astype(jnp.bfloat16)
    grad_values_low = grad_values_two.astype(jnp.bfloat16)
    grad_query_cross = product_left(input_two, grad_queries_two)
    grad_kv_cross = product_left(
        text_states, jnp.concatenate([grad_keys_low, grad_values_low], axis=1)
    )
    text_grad = product_right(grad_keys_low, key_cross) + product_right(
        grad_values_low, value_cross
    )
    grad_part, grad_gain_cross = norm_back(
        product_right(grad_queries_two, query_cross),
        plain_two,
        inverse_two,
        gain_cross.astype(jnp.float32),
    )
    grad_self = grad_cross + grad_part
    shard_qo_cross = reduce_shards(
        by_owner(jnp.concatenate([grad_query_cross, grad_out_cross], axis=1).astype(jnp.bfloat16))
    )
    shard_kv_cross = reduce_shards(by_owner(grad_kv_cross.astype(jnp.bfloat16)), True)
    grad_low_one = grad_self.astype(jnp.bfloat16)
    grad_out_self = product_left(mixture_one, grad_low_one)
    shard_out_self = reduce_shards(by_owner(grad_out_self.astype(jnp.bfloat16)))
    grad_mix_one = product_right(grad_low_one, out_self).astype(jnp.bfloat16)
    query_parts = []
    grad_keys_one = jnp.zeros(keys_one.shape, jnp.float32)
    grad_values_one = jnp.zeros(values_one.shape, jnp.float32)
    for (row_begin, row_end), log_total in zip(blocks, totals_one):
        allowed = self_mask(positions, item_of, row_begin, row_end)
        block_q_grad, block_k_grad, block_v_grad = attend_back(
            queries_one[row_begin:row_end],
            keys_one[:row_end],
            values_one[:row_end],
            allowed,
            log_total,
            grad_mix_one[row_begin:row_end],
        )
        query_parts.append(block_q_grad)
        grad_keys_one = grad_keys_one.at[:row_end].add(block_k_grad)
        grad_values_one = grad_values_one.at[:row_end].add(block_v_grad)
    grad_queries_one = jnp.concatenate(query_parts, axis=0).astype(jnp.bfloat16)
    grad_keys_low = grad_keys_one.astype(jnp.bfloat16)
    grad_values_low = grad_values_one.astype(jnp.bfloat16)
    grad_low_all = jnp.concatenate([grad_queries_one, grad_keys_low, grad_values_low], axis=1)
    grad_qkv_self = product_left(input_one, grad_low_all).astype(jnp.bfloat16)
    half = grad_qkv_self.shape[1] // 2
    shard_qkv_low = reduce_shards(by_owner(grad_qkv_self[:, :half]))
    shard_qkv_high = reduce_shards(by_owner(grad_qkv_self[:, half:]), True)
    grad_input_one = product_right(grad_low_all, qkv_self)
    grad_part, grad_gain_self = norm_back(
        grad_input_one, plain_one, inverse_one, gain_self.astype(jnp.float32)
    )
    hidden_grad = grad_self + grad_part
    shard_small = reduce_shards(
        jnp.concatenate(
            [
                by_owner(grad)
                for grad in (
                    grad_gain_self,
                    grad_gain_cross,
                    grad_gain_mlp,
                    grad_bias_in,
                    grad_bias_out,
                )
            ],
            axis=1,
        )[:, None]
    )[0]
    small_shards = [shard_small[low:high] for low, high in zip(cuts[:-1], cuts[1:])]
    shard_qkv = jnp.concatenate([shard_qkv_low, shard_qkv_high], axis=1)
    return (
        block_out,
        hidden_grad,
        text_grad,
        small_shards[0],
        shard_qkv[:, :width],
        shard_qkv[:, width : 2 * width],
        shard_qkv[:, 2 * width :],
        shard_out_self,
        small_shards[1],
        shard_qo_cross[:, :width],
        shard_kv_cross[:, :width],
        shard_kv_cross[:, width:],
        shard_qo_cross[:, width:],
        small_shards[2],
        shard_in_mlp,
        small_shards[3],
        shard_out_mlp,
        small_shards[4],
    )


def solution(mesh):
    return jax.shard_map(
        local,
        mesh=mesh,
        in_specs=(
            P(("dp", "fsdp"), None),
            P(("dp", "fsdp"), None),
            P(("dp", "fsdp")),
            P(("dp", "fsdp"), None),
            P(("dp", "fsdp"), None),
            P(("dp", "fsdp")),
            P(("dp", "fsdp"), None),
            P(("dp", "fsdp"), None),
            P(("dp", "fsdp"), None),
            P(("dp", "fsdp"), None),
            P(("dp", "fsdp")),
            P(("dp", "fsdp"), None),
            P(("dp", "fsdp"), None),
            P(("dp", "fsdp"), None),
            P(("dp", "fsdp"), None),
            P(("dp", "fsdp")),
            P(("dp", "fsdp"), None),
            P(("dp", "fsdp")),
            P(("dp", "fsdp"), None),
            P(("dp", "fsdp")),
        ),
        out_specs=(
            P(("dp", "fsdp"), None),
            P(("dp", "fsdp"), None),
            P(("dp", "fsdp"), None),
            P(("dp", "fsdp")),
            P(("dp", "fsdp"), None),
            P(("dp", "fsdp"), None),
            P(("dp", "fsdp"), None),
            P(("dp", "fsdp"), None),
            P(("dp", "fsdp")),
            P(("dp", "fsdp"), None),
            P(("dp", "fsdp"), None),
            P(("dp", "fsdp"), None),
            P(("dp", "fsdp"), None),
            P(("dp", "fsdp")),
            P(("dp", "fsdp"), None),
            P(("dp", "fsdp")),
            P(("dp", "fsdp"), None),
            P(("dp", "fsdp")),
        ),
        check_vma=False,
    )
```
